32 devices in a mesh: replica: 8 (over y, x, core), shard: 4 (over z).
Axes of the slice: x: 2, y: 2, z: 4, core: 2. Of those that a mesh axis runs over, the one named last changes fastest.
Arguments:
- tokens: bfloat16 [4096, 768], P(('replica', 'shard')), may hold values from -5 to 5
- cotangent: bfloat16 [4096, 768], P(('replica', 'shard')), may hold values from -6 to 6
- routes: int32 [4096, 2], P(('replica', 'shard')), may hold values from 0 to 63, all different within a row; in each aligned block of 128 rows (0 to 127, 128 to 255, ...) at most 5 rows name the same one
- qkv_weight: bfloat16 [768, 2304], P('shard'), may hold values from -0.15335867 to 0.15335867
- out_weight: bfloat16 [768, 768], P('shard'), may hold values from -1.75 to 1.75
- router_weight: bfloat16 [768, 64], P('shard'), may hold values from -0.21875 to 0.21875
- attn_gain: bfloat16 [768], P('shard'), may hold values from 0.5 to 1.5
- moe_gain: bfloat16 [768], P('shard'), may hold values from 0.5 to 1.5
- bias_table: bfloat16 [32, 12], P('shard'), may hold values from -4 to 4
- expert_in: bfloat16 [64, 768, 3072], P('shard', None, 'replica'), may hold values from -0.21875 to 0.21875
- expert_out: bfloat16 [64, 3072, 768], P('shard', 'replica'), may hold values from -0.109375 to 0.109375
Outputs:
- layer_out: float32 [4096, 768], P(('replica', 'shard'))
- grad_tokens: float32 [4096, 768], P(('replica', 'shard'))
- grad_qkv_weight: float32 [768, 2304], P('shard')
- grad_out_weight: float32 [768, 768], P('shard')
- grad_router_weight: float32 [768, 64], P('shard')
- grad_attn_gain: float32 [768], P('shard')
- grad_moe_gain: float32 [768], P('shard')
- grad_bias_table: float32 [32, 12], P('shard')
- grad_expert_in: float32 [64, 768, 3072], P('shard', None, 'replica')
- grad_expert_out: float32 [64, 3072, 768], P('shard', 'replica')
The draws below stay inside these ranges and needn't reach their ends.
Inputs may be any that keep to these rules, and one draw needn't show every extreme that they name: Among the 256 routes of one device's 128 tokens no expert is named more than 5 times, a bound that some block reaches; the two experts of a token differ.
All inputs are finite; a program needn't handle non-finite values.
Results may differ from the reference program's by a relative error of at most 0.023.
Values may be sent and summed in bfloat16 or wider, within the bound.
No kernel may reach another device: no remote copies, remote signals or barrier semaphores. Data moves between devices by JAX's collectives and lax.ppermute only.
A program may use at most 192 MiB of HBM per device.

```python
import math
import jax
import jax.numpy as jnp
import numpy as np
from jax import lax

D = 768
HEADS = 12
HEAD_DIM = 64
FF = 3072
EXPERTS = 64
BUCKETS = 32
TOK_DEV = 128
CAP = 5
SEQ_LEN = 512
TOKENS = 4096


def drawn_signs(key):
    feature_signs = jax.random.randint(jax.random.fold_in(key, 101), (D,), 0, 2).astype(jnp.float32) * 2.0 - 1.0
    column_signs = jax.random.randint(jax.random.fold_in(key, 102), (D,), 0, 2).astype(jnp.float32) * 2.0 - 1.0
    return (feature_signs, column_signs)


def draw_tokens(key, part):
    feature_signs, column_signs = drawn_signs(key)
    drawn = jax.random.truncated_normal(jax.random.fold_in(key, 1), -5.0, 5.0, (TOKENS, D), jnp.float32)
    chosen = jax.random.randint(jax.random.fold_in(key, 2), (TOKENS,), 0, 32) == 0
    amplitude = jax.random.uniform(jax.random.fold_in(key, 3), (TOKENS, 1), jnp.float32, 1.8, 2.2)
    planted = amplitude * feature_signs[None, :] + jax.random.truncated_normal(jax.random.fold_in(key, 4), -2.5, 2.5, (TOKENS, D), jnp.float32)
    return jnp.where(chosen[:, None], planted, drawn).astype(jnp.bfloat16)


def draw_qkv_weight(key, part):
    feature_signs, column_signs = drawn_signs(key)
    base = jax.random.truncated_normal(jax.random.fold_in(key, 1), -4.0, 4.0, (D, 3 * D), jnp.float32)
    strength = jax.random.uniform(jax.random.fold_in(key, 103), (HEADS,), jnp.float32, 1.15, 1.75)
    per_column = jnp.repeat(strength, HEAD_DIM) * column_signs / math.sqrt(HEAD_DIM)
    planted = (feature_signs / math.sqrt(D))[:, None] * per_column[None, :]
    plant_full = jnp.concatenate([planted, planted, jnp.zeros((D, D), jnp.float32)], axis=1)
    return (base / math.sqrt(D) + plant_full).astype(jnp.bfloat16)


def block_levels(stream_key, extent, split, least, top_value):
    level, own = 1.0, jax.random.fold_in(stream_key, 6)
    for dim, shards_of in split:
        steps = jnp.exp(jax.random.uniform(jax.random.fold_in(own, dim), (shards_of,), jnp.float32, least / len(split), top_value / len(split)))
        level = level * jnp.repeat(steps, extent[dim] // shards_of).reshape([-1 if axis == dim else 1 for axis in range(len(extent))])
    return level


def deal_out(key, own, number, rows, amount, top, limit, lean):
    sequence = jax.random.permutation(key, amount)
    packed, usual = load_shares(amount, rows * top, limit, lean, True), load_shares(amount, rows * top, limit, lean, False)
    places = jnp.arange(amount)

    def named(tallies, turn):
        used = int((tallies > 0).sum())
        fixed = max(1, used // 4)
        passed = fixed + (places - fixed + turn * (used - fixed)) % max(1, amount - fixed)
        return jnp.zeros((amount,), jnp.int32).at[sequence[jnp.where(places < fixed, places, passed)]].set(jnp.asarray(tallies, jnp.int32))

    tallies = jnp.where(number % 4 == 0, named(packed, number // 4), named(usual, number - number // 4 - 1))
    mixed = jax.random.permutation(jax.random.fold_in(own, 3), amount)
    giver, sink = mixed[0:amount // 2 * 2:2], mixed[1:amount // 2 * 2:2]
    room = jnp.minimum(tallies[giver] - 1, limit - tallies[sink]) // 2
    room = jnp.where((giver == sequence[0]) | (sink == sequence[0]) | (tallies[sink] == 0), 0, jnp.maximum(room, 0))
    passed = jax.random.randint(jax.random.fold_in(own, 4), (amount // 2,), 0, 1 << 20) % (room + 1)
    tallies = tallies.at[giver].add(-passed).at[sink].add(passed)
    labels = jnp.searchsorted(jnp.cumsum(tallies), jnp.arange(rows * top), side="right").astype(jnp.int32)
    table = labels.reshape(top, rows).T
    table = table[jax.random.permutation(jax.random.fold_in(own, 1), rows)]
    turn = jax.random.randint(jax.random.fold_in(own, 2), (rows, 1), 0, top)
    return jnp.take_along_axis(table, (jnp.arange(top)[None, :] + turn) % top, axis=1)


def load_shares(number_of, total, most, lean, full):
    portions = [(1 << 20) // math.isqrt(rank ** lean) + 1 for rank in range(1, number_of + 1)]
    largest = most if full else min(most, max(-(-total // number_of), total * portions[0] // sum(portions)))
    least = 1 if total - largest >= number_of - 1 else 0
    holding, rest = [largest] + [least] * (number_of - 1), total - largest - least * (number_of - 1)
    while rest > 0:
        movable = [i for i in range(1, number_of) if holding[i] < largest] or [i for i in range(1, number_of) if holding[i] < most]
        whole, left = sum([portions[i] for i in movable]), rest
        for i in movable:
            more = min(most - holding[i], max(1, left * portions[i] // whole), rest)
            holding[i] = holding[i] + more
            rest = rest - more
    return np.array(holding)


def scatter_about(rng, extent, scale, reach, split=(), kind=jnp.bfloat16):
    values = scale * jax.random.normal(rng, extent, jnp.float32)
    if split:
        values = values * block_levels(rng, extent, split, -0.22, 0.18)
    return jnp.clip(values, -reach, reach).astype(kind)


def setup_inputs(seed: int = 0) -> dict:
    seeds = jax.random.split(jax.random.key(seed), 12)
    tokens = draw_tokens(jax.random.fold_in(seeds[11], 71), 0)
    cotangent = scatter_about(seeds[1], (TOKENS, D), 1.0, 6.0, ((0, 32),))
    routes_keys = jax.random.split(jax.random.fold_in(seeds[2], 1), TOKENS // TOK_DEV)
    routes_turns = jax.random.permutation(jax.random.fold_in(seeds[2], 3), TOKENS // TOK_DEV)
    routes = jax.vmap(lambda own, number: deal_out(jax.random.fold_in(seeds[2], 2), own, number, TOK_DEV, EXPERTS, 2, CAP, 1))(routes_keys, routes_turns).reshape((TOKENS, 2))
    qkv_weight = draw_qkv_weight(jax.random.fold_in(seeds[11], 71), 0)
    out_weight = scatter_about(seeds[4], (D, D), (D // 64) ** -0.5, 1.75, ((0, 4),))
    router_weight = scatter_about(seeds[5], (D, EXPERTS), D ** -0.5, 0.21875, ((0, 4),))
    attn_gain = jnp.clip(1.0 + 0.1 * jax.random.normal(seeds[6], (D,), jnp.float32), 0.5, 1.5).astype(jnp.bfloat16)
    moe_gain = jnp.clip(1.0 + 0.1 * jax.random.normal(seeds[7], (D,), jnp.float32), 0.5, 1.5).astype(jnp.bfloat16)
    bias_table = scatter_about(seeds[8], (BUCKETS, HEADS), 1.0, 4.0, ((0, 4),))
    expert_in = scatter_about(seeds[9], (EXPERTS, D, FF), D ** -0.5, 0.21875, ((0, 4), (2, 8)))
    expert_out = scatter_about(seeds[10], (EXPERTS, FF, D), FF ** -0.5, 0.109375, ((0, 4), (1, 8)))
    return dict(tokens=tokens, cotangent=cotangent, routes=routes, qkv_weight=qkv_weight, out_weight=out_weight, router_weight=router_weight, attn_gain=attn_gain, moe_gain=moe_gain, bias_table=bias_table, expert_in=expert_in, expert_out=expert_out)


bucket_edges = list(range(1, 16)) + [int(math.ceil(16.0 * 8.0 ** (step_m / 16.0))) for step_m in range(16)]
epsilon = 1e-06
negative = -1e+30

def bucket_of(distance):
    bucket_ids = jnp.zeros(distance.shape, jnp.int32)
    for bucket_edge in bucket_edges:
        bucket_ids = bucket_ids + (distance >= bucket_edge).astype(jnp.int32)
    return bucket_ids

def gelu_tanh(pre_act):
    return jax.nn.gelu(pre_act, approximate=True)

def round_half(values):
    return lax.optimization_barrier(values.astype(jnp.bfloat16)).astype(jnp.float32)

def rms_forward(values, gain_vec):
    inv_scale = lax.rsqrt(lax.optimization_barrier(jnp.mean(values * values, axis=-1, keepdims=True)) + epsilon)
    return (inv_scale, values * inv_scale * gain_vec)

def rms_backward(values, inv_scale, gain_vec, grad_normed):
    weighted = grad_normed * gain_vec
    cube = inv_scale * inv_scale * inv_scale
    grad_values = inv_scale * weighted - values * cube * lax.optimization_barrier(jnp.mean(weighted * values, axis=-1, keepdims=True))
    grad_gain = lax.optimization_barrier(jnp.sum(grad_normed * values * inv_scale, axis=0))
    return (grad_values, grad_gain)

def diagonal_sums(grad_scores):
    head_count, row_count, col_count = grad_scores.shape
    flipped = grad_scores[:, :, ::-1]
    padded = jnp.pad(flipped, ((0, 0), (0, 0), (0, row_count)))
    width = col_count + row_count - 1
    skewed = padded.reshape(head_count, row_count * (col_count + row_count))[:, :row_count * width].reshape(head_count, row_count, width)
    return lax.optimization_barrier(jnp.sum(skewed, axis=1))

def bucket_sums(diagonal, distance, bucket_count):
    valid = distance >= 0
    bucket_ids = bucket_of(jnp.maximum(distance, 0))
    table = ((bucket_ids[:, None] == jnp.arange(bucket_count, dtype=jnp.int32)[None, :]) & valid[:, None]).astype(jnp.float32)
    return jnp.einsum('hc,cb->bh', diagonal, table, precision=lax.Precision.HIGHEST)

def block_scores(query_rows, key_rows, bias_heads, row_start):
    row_count = query_rows.shape[0]
    col_count = key_rows.shape[0]
    query3 = query_rows.astype(jnp.float32).reshape(row_count, HEADS, HEAD_DIM)
    key3 = key_rows.astype(jnp.float32).reshape(col_count, HEADS, HEAD_DIM)
    scores = jnp.einsum('qhd,khd->hqk', query3, key3)
    distance = (row_start + jnp.arange(row_count, dtype=jnp.int32))[:, None] - jnp.arange(col_count, dtype=jnp.int32)[None, :]
    allowed = distance >= 0
    clipped = jnp.clip(distance, 0, col_count - 1)
    return (scores + jnp.take(bias_heads, clipped, axis=1), allowed)

def reference(tokens, cotangent, routes, qkv_weight, out_weight, router_weight, attn_gain, moe_gain, bias_table, expert_in, expert_out):
    residual = tokens.astype(jnp.float32)
    gain_one = attn_gain.astype(jnp.float32)
    gain_two = moe_gain.astype(jnp.float32)
    qscale = 1.0 / math.sqrt(HEAD_DIM)
    inv_one, normed = rms_forward(residual, gain_one)
    normed_one = normed.astype(jnp.bfloat16)
    projected = jnp.dot(normed_one, qkv_weight, preferred_element_type=jnp.float32)
    query_all = (projected[:, :D] * qscale).astype(jnp.bfloat16)
    key_all = projected[:, D:2 * D].astype(jnp.bfloat16)
    value_all = projected[:, 2 * D:].astype(jnp.bfloat16)
    bucket_dist = bucket_of(jnp.arange(SEQ_LEN, dtype=jnp.int32))
    bias_heads = jnp.transpose(bias_table.astype(jnp.float32))[:, bucket_dist]
    q_block = min(512, SEQ_LEN)
    block_count = SEQ_LEN // q_block
    seq_count = TOKENS // SEQ_LEN
    block_starts = jnp.arange(block_count, dtype=jnp.int32) * q_block

    def attend_sequence(pieces):
        query_seq, key_seq, value_seq = pieces
        value3 = value_seq.astype(jnp.float32).reshape(SEQ_LEN, HEADS, HEAD_DIM)

        def attend_block(block_pieces):
            query_blk, row_start = block_pieces
            scores, allowed = block_scores(query_blk, key_seq, bias_heads, row_start)
            row_peak = lax.optimization_barrier(jnp.max(jnp.where(allowed, scores, negative), axis=2, keepdims=True))
            row_total = lax.optimization_barrier(jnp.sum(jnp.where(allowed, jnp.exp(scores - row_peak), 0.0), axis=2, keepdims=True))
            log_total = row_peak + jnp.log(row_total)
            weights = round_half(jnp.where(allowed, jnp.exp(scores - log_total), 0.0))
            attended = jnp.einsum('hqk,khd->qhd', weights, value3).reshape(q_block, D)
            return (attended, log_total[:, :, 0])
        return lax.map(attend_block, (query_seq.reshape(block_count, q_block, D), block_starts))
    seq_shape = (seq_count, SEQ_LEN, D)
    attended_all, lse_all = lax.map(attend_sequence, (query_all.reshape(seq_shape), key_all.reshape(seq_shape), value_all.reshape(seq_shape)))
    attended_f = attended_all.reshape(TOKENS, D)
    attended_b = attended_f.astype(jnp.bfloat16)
    hidden = residual + jnp.dot(attended_b, out_weight, preferred_element_type=jnp.float32)
    inv_two, normed = rms_forward(hidden, gain_two)
    normed_two = normed.astype(jnp.bfloat16)
    logits = jnp.dot(normed_two, router_weight, preferred_element_type=jnp.float32)
    route_hits = routes[:, :, None] == jnp.arange(EXPERTS, dtype=jnp.int32)[None, None, :]
    picked = lax.optimization_barrier(jnp.sum(jnp.where(route_hits, logits[:, None, :], 0.0), axis=2))
    margin = picked[:, 0] - picked[:, 1]
    gate_probs = jnp.stack([jax.nn.sigmoid(margin), jax.nn.sigmoid(-margin)], axis=1)
    dev_count = TOKENS // TOK_DEV
    per_dev = 2 * TOK_DEV
    flat_routes = routes.reshape(dev_count, per_dev)
    hits_int = (flat_routes[:, :, None] == jnp.arange(EXPERTS, dtype=jnp.int32)[None, None, :]).astype(jnp.int32)
    rank = lax.optimization_barrier(jnp.sum(jnp.cumsum(hits_int, axis=1) * hits_int, axis=2)) - 1
    slot_width = dev_count * CAP
    route_slot = (flat_routes * slot_width + jnp.arange(dev_count, dtype=jnp.int32)[:, None] * CAP + rank).reshape(-1)
    route_total = 2 * TOKENS
    slot_route = jnp.full((EXPERTS * slot_width,), route_total, jnp.int32).at[route_slot].set(jnp.arange(route_total, dtype=jnp.int32))

    def slot_rows(route_rows):
        padded = jnp.concatenate([route_rows, jnp.zeros((1, D), route_rows.dtype)], axis=0)
        return padded[slot_route].reshape(EXPERTS, slot_width, D)
    expert_rows = slot_rows(jnp.repeat(normed_two, 2, axis=0))

    def expert_forward(pieces):
        rows_in, weight_in, weight_out = pieces
        activated = gelu_tanh(jnp.dot(rows_in, weight_in, preferred_element_type=jnp.float32)).astype(jnp.bfloat16)
        return jnp.dot(activated, weight_out, preferred_element_type=jnp.float32).astype(jnp.bfloat16)
    expert_result = lax.map(expert_forward, (expert_rows, expert_in, expert_out)).reshape(EXPERTS * slot_width, D)
    route_out = expert_result[route_slot].astype(jnp.float32).reshape(TOKENS, 2, D)
    layer_out = hidden + lax.optimization_barrier(jnp.sum(gate_probs[:, :, None] * route_out, axis=1))
    grad_out = cotangent.astype(jnp.float32)
    grad_gate = lax.optimization_barrier(jnp.sum(grad_out[:, None, :] * route_out, axis=2))
    grad_picked = gate_probs * (grad_gate - lax.optimization_barrier(jnp.sum(gate_probs * grad_gate, axis=1, keepdims=True)))
    grad_logits = lax.optimization_barrier(jnp.sum(jnp.where(route_hits, grad_picked[:, :, None], 0.0), axis=1))
    grad_route_rows = (gate_probs[:, :, None] * grad_out[:, None, :]).reshape(route_total, D).astype(jnp.bfloat16)
    grad_expert_rows = slot_rows(grad_route_rows)

    def expert_backward(pieces):
        rows_in, grad_rows, weight_in, weight_out = pieces
        pre_act = jnp.dot(rows_in, weight_in, preferred_element_type=jnp.float32)
        activated, gelu_pullback = jax.vjp(gelu_tanh, pre_act)
        grad_act = jnp.dot(grad_rows, weight_out.T, preferred_element_type=jnp.float32)
        grad_pre = gelu_pullback(grad_act)[0].astype(jnp.bfloat16)
        grad_weight_out = jnp.dot(activated.astype(jnp.bfloat16).T, grad_rows, preferred_element_type=jnp.float32)
        grad_weight_in = jnp.dot(rows_in.T, grad_pre, preferred_element_type=jnp.float32)
        grad_rows_in = jnp.dot(grad_pre, weight_in.T, preferred_element_type=jnp.float32).astype(jnp.bfloat16)
        return (grad_rows_in, grad_weight_in, grad_weight_out)
    grad_slots, grad_expert_in, grad_expert_out = lax.map(expert_backward, (expert_rows, grad_expert_rows, expert_in, expert_out))
    grad_from_experts = grad_slots.reshape(EXPERTS * slot_width, D)[route_slot].astype(jnp.float32).reshape(TOKENS, 2, D)
    router_float = router_weight.astype(jnp.float32)
    grad_normed_two = lax.optimization_barrier(jnp.sum(grad_from_experts, axis=1)) + jnp.dot(grad_logits, router_float.T, precision=lax.Precision.HIGHEST)
    grad_router_weight = jnp.dot(normed_two.astype(jnp.float32).T, grad_logits, precision=lax.Precision.HIGHEST)
    grad_hidden_norm, grad_moe_gain = rms_backward(hidden, inv_two, gain_two, grad_normed_two)
    grad_hidden = grad_out + grad_hidden_norm
    grad_branch = grad_hidden.astype(jnp.bfloat16)
    grad_out_weight = jnp.dot(attended_b.T, grad_branch, preferred_element_type=jnp.float32)
    grad_attended = jnp.dot(grad_branch, out_weight.T, preferred_element_type=jnp.float32).astype(jnp.bfloat16)
    diag_width = q_block + SEQ_LEN - 1

    def grad_sequence(pieces):
        query_seq, key_seq, value_seq, grad_seq, attended_seq, lse_seq = pieces
        key3 = key_seq.astype(jnp.float32).reshape(SEQ_LEN, HEADS, HEAD_DIM)
        value3 = value_seq.astype(jnp.float32).reshape(SEQ_LEN, HEADS, HEAD_DIM)

        def grad_block(running, block_pieces):
            grad_keys, grad_values, grad_table = running
            query_blk, grad_blk, attended_blk, lse_blk, row_start = block_pieces
            scores, allowed = block_scores(query_blk, key_seq, bias_heads, row_start)
            weights = jnp.where(allowed, jnp.exp(scores - lse_blk[:, :, None]), 0.0)
            weights_b = round_half(weights)
            grad3 = grad_blk.astype(jnp.float32).reshape(q_block, HEADS, HEAD_DIM)
            query3 = query_blk.astype(jnp.float32).reshape(q_block, HEADS, HEAD_DIM)
            delta = jnp.transpose(lax.optimization_barrier(jnp.sum(grad3 * attended_blk.reshape(q_block, HEADS, HEAD_DIM), axis=2)))
            grad_weights = jnp.einsum('qhd,khd->hqk', grad3, value3)
            grad_scores = weights * (grad_weights - delta[:, :, None])
            grad_scores_b = round_half(grad_scores)
            grad_query = jnp.einsum('hqk,khd->qhd', grad_scores_b, key3).reshape(q_block, D)
            grad_keys = grad_keys + jnp.einsum('hqk,qhd->khd', grad_scores_b, query3).reshape(SEQ_LEN, D)
            grad_values = grad_values + jnp.einsum('hqk,qhd->khd', weights_b, grad3).reshape(SEQ_LEN, D)
            distance = row_start - (SEQ_LEN - 1) + jnp.arange(diag_width, dtype=jnp.int32)
            grad_table = grad_table + bucket_sums(diagonal_sums(grad_scores), distance, BUCKETS)
            return ((grad_keys, grad_values, grad_table), grad_query)
        start_state = (jnp.zeros((SEQ_LEN, D), jnp.float32), jnp.zeros((SEQ_LEN, D), jnp.float32), jnp.zeros((BUCKETS, HEADS), jnp.float32))
        block_pieces = (query_seq.reshape(block_count, q_block, D), grad_seq.reshape(block_count, q_block, D), attended_seq.reshape(block_count, q_block, D), lse_seq, block_starts)
        (grad_keys, grad_values, grad_table), grad_query = lax.scan(grad_block, start_state, block_pieces)
        return (grad_query.reshape(SEQ_LEN, D), grad_keys, grad_values, grad_table)
    grad_query, grad_keys, grad_values, grad_tables = lax.map(grad_sequence, (query_all.reshape(seq_shape), key_all.reshape(seq_shape), value_all.reshape(seq_shape), grad_attended.reshape(seq_shape), attended_f.reshape(seq_shape), lse_all))
    grad_bias_table = lax.optimization_barrier(jnp.sum(grad_tables, axis=0))
    grad_projected = jnp.concatenate([grad_query.reshape(TOKENS, D) * qscale, grad_keys.reshape(TOKENS, D), grad_values.reshape(TOKENS, D)], axis=1).astype(jnp.bfloat16)
    grad_qkv_weight = jnp.dot(normed_one.T, grad_projected, preferred_element_type=jnp.float32)
    grad_normed_one = jnp.dot(grad_projected, qkv_weight.T, preferred_element_type=jnp.float32)
    grad_resid, grad_attn_gain = rms_backward(residual, inv_one, gain_one, grad_normed_one)
    grad_tokens = grad_hidden + grad_resid
    return (layer_out, grad_tokens, grad_qkv_weight, grad_out_weight, grad_router_weight, grad_attn_gain, grad_moe_gain, grad_bias_table, grad_expert_in, grad_expert_out)
```

```python
import math

import jax
import jax.numpy as jnp
from jax import lax
from jax.experimental import pallas as pl
from jax.experimental.pallas import tpu as pltpu
from jax.sharding import PartitionSpec as P

CAP = 5
BLOCK = 128
VMEM_LIMIT = 60 * 1024 * 1024

bucket_edges = list(range(1, 16)) + [
    int(math.ceil(16.0 * 8.0 ** (step_m / 16.0))) for step_m in range(16)
]
epsilon = 1e-06
negative = -1e30
f32 = jnp.float32
bf16 = jnp.bfloat16


def dot(left, right, left_axis=1, right_axis=0, precision=None):
    return lax.dot_general(
        left,
        right,
        (((left_axis,), (right_axis,)), ((), ())),
        precision=precision,
        preferred_element_type=f32,
    )


def swap(values, axis, bit):
    count = lax.axis_size(axis)
    return lax.ppermute(values, axis, [(i, i ^ bit) for i in range(count)])


def bits_of(count):
    return [1 << i for i in reversed(range(count.bit_length() - 1))]


def add_half(left, right):
    if left.dtype == f32:
        return left + right
    return (left.astype(f32) + right.astype(f32)).astype(left.dtype)


def exchange(blocks):
    return [blocks[0]] + [swap(blocks[k], "shard", k) for k in range(1, len(blocks))]


def gather_relative(values, order):
    held = values[None]
    for bit in order:
        held = jnp.concatenate([held, swap(held, "replica", bit)], axis=0)
    return held


def scatter_relative(values, order):
    for bit in reversed(order):
        half = values.shape[0] // 2
        values = add_half(values[:half], swap(values[half:], "replica", bit))
    return values[0]


def reduce_rows(values):
    me = lax.axis_index("replica")
    count = values.shape[0]
    bit = 1
    while bit < count:
        pairs = values.reshape((values.shape[0] // 2, 2) + values.shape[1:])
        low, high = pairs[:, 0], pairs[:, 1]
        upper = (me & bit) != 0
        values = add_half(
            jnp.where(upper, high, low), swap(jnp.where(upper, low, high), "replica", bit)
        )
        bit *= 2
    return values[0]


def near_tiles(block_count):
    return [d for d in range(block_count) if BLOCK * d - (BLOCK - 1) < bucket_edges[-1]]


def tile_distance(d):
    row = lax.broadcasted_iota(jnp.int32, (BLOCK, BLOCK), 0)
    col = lax.broadcasted_iota(jnp.int32, (BLOCK, BLOCK), 1)
    return row - col + BLOCK * d


def bias_row(table_ref, head, block, near, tiles):
    parts = []
    for j in range(block + 1):
        d = block - j
        if d < near:
            parts.append(tiles[d])
        else:
            parts.append(
                jnp.full((BLOCK, BLOCK), table_ref[len(bucket_edges), head], f32)
            )
    return parts[0] if len(parts) == 1 else jnp.concatenate(parts, axis=1)


def bias_tiles(table_ref, head, near):
    tiles = []
    for d in range(near):
        dist = tile_distance(d)
        tile = jnp.full((BLOCK, BLOCK), table_ref[0, head], f32)
        for index, edge in enumerate(bucket_edges):
            if edge > BLOCK * d + BLOCK - 1:
                break
            tile = jnp.where(dist >= edge, table_ref[index + 1, head], tile)
        if d == 0:
            tile = jnp.where(dist >= 0, tile, negative)
        tiles.append(tile)
    return tiles


def attention_forward(heads_here, head_dim, qscale, table_ref, x_ref, gain_ref, w_ref,
                      n1_ref, qkv_ref, o_ref, ob_ref, lse_ref):
    seq = x_ref.shape[0]
    blocks = seq // BLOCK
    near = len(near_tiles(blocks))
    x = x_ref[...].astype(f32)
    inv = lax.rsqrt(jnp.mean(x * x, axis=1, keepdims=True) + epsilon)
    n1_ref[...] = (x * inv * gain_ref[...]).astype(bf16)
    wide = 3 * head_dim
    for h in range(heads_here):
        projected = dot(n1_ref[...], w_ref[:, h * wide : (h + 1) * wide])
        query = (projected[:, :head_dim] * qscale).astype(bf16)
        key = projected[:, head_dim : 2 * head_dim].astype(bf16)
        value = projected[:, 2 * head_dim :].astype(bf16)
        qkv_ref[h, :, :] = jnp.concatenate([query, key, value], axis=1)
        tiles = bias_tiles(table_ref, h, near)
        for i in range(blocks):
            span = (i + 1) * BLOCK
            rows = slice(i * BLOCK, span)
            scores = dot(query[rows], key[:span], 1, 1) + bias_row(table_ref, h, i, near, tiles)
            peak = jnp.max(scores, axis=1, keepdims=True)
            weights = jnp.exp(scores - peak)
            total = jnp.sum(weights, axis=1, keepdims=True)
            weights = (weights * (1.0 / total)).astype(bf16)
            attended = dot(weights, value[:span])
            o_ref[h, rows, :] = attended
            ob_ref[rows, h * head_dim : (h + 1) * head_dim] = attended.astype(bf16)
            lse_ref[h, rows, :] = jnp.broadcast_to(peak + jnp.log(total), (BLOCK, BLOCK))


def attention_backward(heads_here, head_dim, qscale, table_ref, x_ref, n1_ref, qkv_ref, o_ref,
                       lse_ref, do_ref, w_ref, gw_ref, dn1_ref, gain_ref, tab_ref,
                       dk_ref, dv_ref, dq_ref, acc_ref):
    seq = x_ref.shape[0]
    blocks = seq // BLOCK
    near = len(near_tiles(blocks))
    wide = 3 * head_dim
    bucket_count = len(bucket_edges) + 1
    for h in range(heads_here):
        query = qkv_ref[h, :, :head_dim]
        key = qkv_ref[h, :, head_dim : 2 * head_dim]
        value = qkv_ref[h, :, 2 * head_dim :]
        grad = do_ref[:, h * head_dim : (h + 1) * head_dim]
        tiles = bias_tiles(table_ref, h, near)
        sums = [jnp.zeros((BLOCK, BLOCK), f32) for _ in range(near + 1)]
        dk_ref[...] = jnp.zeros_like(dk_ref)
        dv_ref[...] = jnp.zeros_like(dv_ref)
        for i in range(blocks):
            span = (i + 1) * BLOCK
            rows = slice(i * BLOCK, span)
            q_i, g_i = query[rows], grad[rows]
            scores = dot(q_i, key[:span], 1, 1) + bias_row(table_ref, h, i, near, tiles)
            weights = jnp.exp(scores - lse_ref[h, rows, :][:, :1])
            delta = jnp.sum(g_i.astype(f32) * o_ref[h, rows, :], axis=1, keepdims=True)
            grad_scores = weights * (dot(g_i, value[:span], 1, 1) - delta)
            for j in range(i + 1):
                d = min(i - j, near)
                sums[d] = sums[d] + grad_scores[:, j * BLOCK : (j + 1) * BLOCK]
            half = grad_scores.astype(bf16)
            dq_ref[rows, :] = dot(half, key[:span])
            dk_ref[:span, :] += dot(half, q_i, 0, 0)
            dv_ref[:span, :] += dot(weights.astype(bf16), g_i, 0, 0)
        for b in range(bucket_count):
            low = 0 if b == 0 else bucket_edges[b - 1]
            high = bucket_edges[b] if b < len(bucket_edges) else None
            total = jnp.zeros((1, BLOCK), f32)
            for d in range(near):
                if BLOCK * d + BLOCK - 1 < low:
                    continue
                if high is not None and BLOCK * d - (BLOCK - 1) >= high:
                    continue
                dist = tile_distance(d)
                inside = dist >= low
                if high is not None:
                    inside = inside & (dist < high)
                total = total + jnp.sum(jnp.where(inside, sums[d], 0.0), axis=0, keepdims=True)
            if high is None:
                total = total + jnp.sum(sums[near], axis=0, keepdims=True)
            tab_ref[h, b : b + 1, :] = total
        projected = jnp.concatenate(
            [
                (dq_ref[...] * qscale).astype(bf16),
                dk_ref[...].astype(bf16),
                dv_ref[...].astype(bf16),
            ],
            axis=1,
        )
        columns = slice(h * wide, (h + 1) * wide)
        gw_ref[:, columns] = dot(n1_ref[...], projected, 0, 0).astype(bf16)
        part = dot(projected, w_ref[:, columns], 1, 1)
        if h == 0:
            acc_ref[...] = part
        else:
            acc_ref[...] += part
    x = x_ref[...].astype(f32)
    inv = lax.rsqrt(jnp.mean(x * x, axis=1, keepdims=True) + epsilon)
    total = acc_ref[...]
    gain_ref[...] = jnp.sum(total * x * inv, axis=0, keepdims=True)
    dn1_ref[...] = total.astype(bf16)


def expert_step(x_ref, g_ref, gate_ref, win_ref, wout_ref,
                y_ref, dx_ref, dgate_ref, gwin_ref, gwout_ref):
    rows = x_ref.shape[1]
    x = x_ref[0]
    g = g_ref[0]
    w_in = win_ref[0]
    w_out = wout_ref[0]
    same = lax.broadcasted_iota(jnp.int32, (rows, rows), 0) == lax.broadcasted_iota(
        jnp.int32, (rows, rows), 1
    )
    gate = jnp.sum(jnp.where(same, gate_ref[0], 0.0), axis=1, keepdims=True)
    pre = dot(x, w_in)
    c0 = math.sqrt(2.0 / math.pi)
    square = pre * pre
    bent = jnp.tanh(c0 * (pre + 0.044715 * (square * pre)))
    act = (0.5 * pre * (1.0 + bent)).astype(bf16)
    slope = 0.5 * (1.0 + bent) + 0.5 * pre * (1.0 - bent * bent) * (
        c0 * (1.0 + 3.0 * 0.044715 * square)
    )
    back = dot(g, w_out, 1, 1)
    scaled = (gate * g.astype(f32)).astype(bf16)
    dgate = jnp.sum(act.astype(f32) * back, axis=1, keepdims=True)
    dgate_ref[0] = jnp.sum(jnp.where(same, dgate, 0.0), axis=0, keepdims=True)
    dpre = (gate * back * slope).astype(bf16)
    dx_ref[0] = dot(dpre, w_in, 1, 1).astype(bf16)
    y_ref[0] = dot(act, w_out).astype(bf16)
    gwin_ref[0] = dot(x, dpre, 0, 0)
    gwout_ref[0] = dot(act, scaled, 0, 0)


def run_experts(xs, gs, gates, w_in, w_out):
    local, rows, width = xs.shape
    hidden = w_in.shape[2]
    row_spec = pl.BlockSpec((1, rows, width), lambda e: (e, 0, 0))
    gate_spec = pl.BlockSpec((1, 1, rows), lambda e: (e, 0, 0))
    in_spec = pl.BlockSpec((1, width, hidden), lambda e: (e, 0, 0))
    out_spec = pl.BlockSpec((1, hidden, width), lambda e: (e, 0, 0))
    return pl.pallas_call(
        expert_step,
        grid=(local,),
        in_specs=[row_spec, row_spec, gate_spec, in_spec, out_spec],
        out_specs=[row_spec, row_spec, gate_spec, in_spec, out_spec],
        out_shape=[
            jax.ShapeDtypeStruct(xs.shape, bf16),
            jax.ShapeDtypeStruct(xs.shape, bf16),
            jax.ShapeDtypeStruct((local, 1, rows), f32),
            jax.ShapeDtypeStruct(w_in.shape, f32),
            jax.ShapeDtypeStruct(w_out.shape, f32),
        ],
        compiler_params=pltpu.CompilerParams(
            dimension_semantics=("arbitrary",), vmem_limit_bytes=VMEM_LIMIT
        ),
        cost_estimate=pl.CostEstimate(
            flops=12 * local * rows * width * hidden,
            transcendentals=local * rows * hidden,
            bytes_accessed=12 * local * width * hidden + 8 * local * rows * width,
        ),
        name="experts",
    )(xs, gs, gates, w_in, w_out)


def body(
    tokens,
    cotangent,
    routes,
    qkv_weight,
    out_weight,
    router_weight,
    attn_gain,
    moe_gain,
    bias_table,
    expert_in,
    expert_out,
):
    shards = lax.axis_size("shard")
    replicas = lax.axis_size("replica")
    me_shard = lax.axis_index("shard")
    me_replica = lax.axis_index("replica")
    tok_rows, width = tokens.shape
    seq_len = tok_rows * shards
    table_rows, head_count = bias_table.shape
    bucket_count = table_rows * shards
    head_dim = width // head_count
    heads_here = -(-head_count // shards)
    head_pad = heads_here * shards - head_count
    wide = 3 * head_dim
    experts = router_weight.shape[1]
    local = expert_in.shape[0]
    dense_rows = width // shards
    piece = dense_rows // replicas
    qscale = 1.0 / math.sqrt(head_dim)
    highest = lax.Precision.HIGHEST
    order_a = bits_of(replicas)
    order_b = order_a[:-1][::-1] + order_a[-1:]
    my_piece = me_replica * piece

    hits = routes[:, :, None] == lax.iota(jnp.int32, experts)[None, None, :]
    named = (hits[:, 0] | hits[:, 1]).astype(bf16)
    earlier = (
        lax.iota(jnp.int32, tok_rows)[:, None] > lax.iota(jnp.int32, tok_rows)[None, :]
    ).astype(bf16)
    prior = dot(earlier, named)
    rank = jnp.sum(jnp.where(hits, prior[:, None, :], 0.0), axis=2).astype(jnp.int32)
    slot = (
        ((routes // local) ^ me_shard) * (CAP * local) + rank * local + routes % local
    )
    slot_count = experts * CAP
    slot_iota = lax.iota(jnp.int32, slot_count)[:, None]
    place = [slot_iota == slot[None, :, k] for k in range(2)]
    place_half = [p.astype(bf16) for p in place]
    place_any = place_half[0] + place_half[1]

    def to_blocks(slot_values):
        return [
            slot_values[k * CAP * local : (k + 1) * CAP * local] for k in range(shards)
        ]

    def spread(slot_values):
        blocks = exchange(to_blocks(slot_values))
        half = shards // 2
        parts = []
        for group, order in ((blocks[:half], order_a), (blocks[half:], order_b)):
            held = gather_relative(jnp.concatenate(group, axis=0), order)
            parts.append(held.reshape((replicas * half * CAP, local) + slot_values.shape[1:]))
        return jnp.swapaxes(jnp.concatenate(parts, axis=0), 0, 1)

    def bring(rows):
        flat = jnp.swapaxes(rows, 0, 1)
        half = shards // 2
        count = flat.shape[0] // 2
        blocks = []
        for group, order in ((flat[:count], order_a), (flat[count:], order_b)):
            own = scatter_relative(
                group.reshape((replicas, half * CAP * local) + rows.shape[2:]), order
            )
            blocks += [own[k * CAP * local : (k + 1) * CAP * local] for k in range(half)]
        return jnp.concatenate(exchange(blocks), axis=0)

    grad_rows = spread(dot(place_any, cotangent).astype(bf16))

    small = jnp.zeros((dense_rows, BLOCK), bf16)
    small = small.at[:, :experts].set(router_weight)
    small = small.at[:, experts].set(attn_gain)
    small = small.at[:, experts + 1].set(moe_gain)
    small = small.at[: table_rows * head_count, experts + 2].set(bias_table.reshape(-1))
    small_rows = dense_rows * BLOCK // width
    packed = jnp.concatenate([tokens, small.reshape(small_rows, width)], axis=0)
    packed = lax.all_gather(packed, "shard", axis=0)
    sequence = packed[:, :tok_rows].reshape(seq_len, width)
    small = packed[:, tok_rows:].reshape(width, BLOCK)
    router_full = small[:, :experts]
    gain_one = small[:, experts].astype(f32)[None, :]
    gain_two = small[:, experts + 1].astype(f32)[None, :]
    table_full = (
        small[:, experts + 2]
        .reshape(shards, dense_rows)[:, : table_rows * head_count]
        .reshape(bucket_count, head_count)
        .astype(f32)
    )
    table_pad = jnp.pad(table_full, ((0, 0), (0, head_pad)))
    table_here = lax.dynamic_slice_in_dim(table_pad, me_shard * heads_here, heads_here, 1)

    columns = lax.dynamic_slice_in_dim(qkv_weight, my_piece, piece, 0).reshape(
        piece, 3, head_count, head_dim
    )
    columns = jnp.pad(columns, ((0, 0), (0, 0), (0, head_pad), (0, 0)))
    columns = columns.reshape(piece, 3, shards, heads_here, head_dim)
    columns = jnp.transpose(columns, (2, 0, 3, 1, 4)).reshape(shards, piece, heads_here * wide)
    columns = lax.all_to_all(columns, "shard", split_axis=0, concat_axis=0, tiled=True)
    columns = lax.all_gather(columns, "replica", axis=0)
    qkv_here = jnp.swapaxes(columns, 0, 1).reshape(width, heads_here * wide)
    out_full = lax.all_gather(
        lax.dynamic_slice_in_dim(out_weight, my_piece, piece, 0),
        ("shard", "replica"),
        axis=0,
        tiled=True,
    )

    smem = pl.BlockSpec(memory_space=pltpu.SMEM)
    vmem = pl.BlockSpec(memory_space=pltpu.VMEM)
    attn_flops = heads_here * seq_len * (2 * width * wide + 2 * seq_len * head_dim)
    normed_one, qkv_rows, attended, attended_b, log_total = pl.pallas_call(
        lambda *refs: attention_forward(heads_here, head_dim, qscale, *refs),
        in_specs=[smem, vmem, vmem, vmem],
        out_specs=[vmem] * 5,
        out_shape=[
            jax.ShapeDtypeStruct((seq_len, width), bf16),
            jax.ShapeDtypeStruct((heads_here, seq_len, wide), bf16),
            jax.ShapeDtypeStruct((heads_here, seq_len, head_dim), f32),
            jax.ShapeDtypeStruct((seq_len, heads_here * head_dim), bf16),
            jax.ShapeDtypeStruct((heads_here, seq_len, BLOCK), f32),
        ],
        compiler_params=pltpu.CompilerParams(vmem_limit_bytes=VMEM_LIMIT),
        cost_estimate=pl.CostEstimate(
            flops=attn_flops,
            transcendentals=heads_here * seq_len * seq_len,
            bytes_accessed=8 * seq_len * width,
        ),
        name="attention_forward",
    )(table_here, sequence, gain_one, qkv_here)

    attended_tok = lax.all_to_all(
        attended_b.reshape(shards, tok_rows, heads_here * head_dim),
        "shard",
        split_axis=0,
        concat_axis=0,
        tiled=True,
    )
    attended_tok = jnp.swapaxes(attended_tok, 0, 1).reshape(tok_rows, -1)[:, :width]

    residual = tokens.astype(f32)
    hidden = residual + dot(attended_tok, out_full)
    inv_two = lax.rsqrt(jnp.mean(hidden * hidden, axis=-1, keepdims=True) + epsilon)
    normed_two = (hidden * inv_two * gain_two).astype(bf16)
    logits = dot(normed_two, router_full)
    picked = jnp.sum(jnp.where(hits, logits[:, None, :], 0.0), axis=2)
    margin = picked[:, 0] - picked[:, 1]
    gates = [jax.nn.sigmoid(margin), jax.nn.sigmoid(-margin)]
    gate_slots = jnp.sum(
        jnp.where(place[0], gates[0][None, :], 0.0) + jnp.where(place[1], gates[1][None, :], 0.0),
        axis=1,
    )
    expert_rows = spread(dot(place_any, normed_two).astype(bf16))
    gate_rows = spread(gate_slots)

    y_rows, dx_rows, dgate_rows, grad_expert_in, grad_expert_out = run_experts(
        expert_rows, grad_rows, gate_rows[:, None, :], expert_in, expert_out
    )

    dgate_slots = bring(dgate_rows[:, 0, :])
    dx_slots = bring(dx_rows)
    dgate = [jnp.sum(jnp.where(p, dgate_slots[:, None], 0.0), axis=0) for p in place]
    mean_gate = gates[0] * dgate[0] + gates[1] * dgate[1]
    dpick = jnp.stack([gates[k] * (dgate[k] - mean_gate) for k in range(2)], axis=1)
    grad_logits = jnp.sum(jnp.where(hits, dpick[:, :, None], 0.0), axis=1)
    grad_normed = dot(place_any, dx_slots, 0, 0) + dot(
        grad_logits, router_full.astype(f32), 1, 1, precision=highest
    )
    grad_router = dot(normed_two.astype(f32), grad_logits, 0, 0, precision=highest)
    weighted = grad_normed * gain_two
    grad_out = cotangent.astype(f32)
    grad_hidden = (
        grad_out
        + inv_two * weighted
        - hidden
        * (inv_two * inv_two * inv_two)
        * jnp.mean(weighted * hidden, axis=-1, keepdims=True)
    )
    grad_gain_two = jnp.sum(grad_normed * hidden * inv_two, axis=0)
    grad_branch = grad_hidden.astype(bf16)
    grad_att = dot(grad_branch, out_full, 1, 1).astype(bf16)
    grad_att = jnp.pad(grad_att, ((0, 0), (0, head_pad * head_dim)))
    grad_att = jnp.swapaxes(grad_att.reshape(tok_rows, shards, heads_here * head_dim), 0, 1)
    grad_att = lax.all_to_all(grad_att, "shard", split_axis=0, concat_axis=0, tiled=True)
    grad_att = grad_att.reshape(seq_len, heads_here * head_dim)

    def reduce_dense(values):
        cols = values.shape[1]
        blocks = jnp.swapaxes(values.reshape(shards, replicas, piece, cols), 0, 1)
        own = reduce_rows(blocks.reshape(replicas, shards * piece, cols))
        return lax.all_to_all(
            own.reshape(shards, piece, cols), "shard", split_axis=0, concat_axis=0, tiled=True
        )

    grad_out_weight = dot(attended_tok, grad_branch, 0, 0)
    extra = jnp.concatenate(
        [grad_router, grad_gain_two[:, None], jnp.zeros((width, BLOCK - experts - 1), f32)], axis=1
    )
    dense_two = reduce_dense(jnp.concatenate([grad_out_weight, extra], axis=1).astype(bf16))
    dense_two = jnp.sum(dense_two.astype(f32), axis=0)

    grad_qkv, grad_n1, gain_part, table_part = pl.pallas_call(
        lambda *refs: attention_backward(heads_here, head_dim, qscale, *refs),
        in_specs=[smem] + [vmem] * 7,
        out_specs=[vmem] * 4,
        out_shape=[
            jax.ShapeDtypeStruct((width, heads_here * wide), bf16),
            jax.ShapeDtypeStruct((seq_len, width), bf16),
            jax.ShapeDtypeStruct((1, width), f32),
            jax.ShapeDtypeStruct((heads_here, bucket_count, BLOCK), f32),
        ],
        scratch_shapes=[
            pltpu.VMEM((seq_len, head_dim), f32),
            pltpu.VMEM((seq_len, head_dim), f32),
            pltpu.VMEM((seq_len, head_dim), f32),
            pltpu.VMEM((seq_len, width), f32),
        ],
        compiler_params=pltpu.CompilerParams(vmem_limit_bytes=VMEM_LIMIT),
        cost_estimate=pl.CostEstimate(
            flops=3 * attn_flops,
            transcendentals=heads_here * seq_len * seq_len,
            bytes_accessed=8 * seq_len * width,
        ),
        name="attention_backward",
    )(table_here, sequence, normed_one, qkv_rows, attended, log_total, grad_att, qkv_here)

    grad_n1 = lax.psum_scatter(grad_n1, "shard", scatter_dimension=0, tiled=True).astype(f32)

    table_part = jnp.sum(table_part, axis=2)
    table_column = jnp.zeros((shards, dense_rows), f32)
    table_column = table_column.at[:, : table_rows * heads_here].set(
        jnp.transpose(table_part).reshape(shards, table_rows * heads_here)
    )
    extra = jnp.concatenate(
        [
            gain_part.reshape(width, 1),
            table_column.reshape(width, 1),
            jnp.zeros((width, -(heads_here * wide + 2) % BLOCK), f32),
        ],
        axis=1,
    ).astype(bf16)
    dense_one = reduce_dense(jnp.concatenate([grad_qkv, extra], axis=1))
    own_qkv = dense_one[:, :, : heads_here * wide].reshape(
        shards, piece, heads_here, 3, head_dim
    )
    own_qkv = jnp.transpose(own_qkv, (1, 3, 0, 2, 4)).reshape(piece, 3, -1)[:, :, :width]
    own_extra = dense_one[:, :, heads_here * wide :].astype(f32)
    own_gain = jnp.sum(own_extra[:, :, 0], axis=0)
    own_table = jnp.transpose(own_extra[:, :, 1])
    tail = jnp.concatenate(
        [own_gain[:, None], own_table, jnp.zeros((piece, BLOCK - 1 - shards), f32)], axis=1
    )
    final = jnp.concatenate(
        [own_qkv.reshape(piece, 3 * width), dense_two.astype(bf16), tail.astype(bf16)], axis=1
    )
    final = lax.all_gather(final, "replica", axis=0, tiled=True).astype(f32)
    grad_qkv_weight = final[:, : 3 * width]
    grad_out_weight = final[:, 3 * width : 4 * width]
    final_two = final[:, 4 * width : 4 * width + BLOCK]
    final_one = final[:, 4 * width + BLOCK :]
    grad_router = final_two[:, :experts]
    grad_moe_gain = final_two[:, experts]
    grad_attn_gain = final_one[:, 0]
    grad_table = final_one[: table_rows * heads_here, 1 : 1 + shards]
    grad_table = jnp.transpose(
        grad_table.reshape(table_rows, heads_here, shards), (0, 2, 1)
    ).reshape(table_rows, shards * heads_here)[:, :head_count]

    y_slots = bring(y_rows)
    layer_out = hidden
    for k in range(2):
        layer_out = layer_out + gates[k][:, None] * dot(place_half[k], y_slots, 0, 0)

    inv_one = lax.rsqrt(jnp.mean(residual * residual, axis=-1, keepdims=True) + epsilon)
    weighted = grad_n1 * gain_one
    grad_tokens = (
        grad_hidden
        + inv_one * weighted
        - residual
        * (inv_one * inv_one * inv_one)
        * jnp.mean(weighted * residual, axis=-1, keepdims=True)
    )
    return (
        layer_out,
        grad_tokens,
        grad_qkv_weight,
        grad_out_weight,
        grad_router,
        grad_attn_gain,
        grad_moe_gain,
        grad_table,
        grad_expert_in,
        grad_expert_out,
    )


def solution(mesh):
    return jax.shard_map(
        body,
        mesh=mesh,
        in_specs=(
            P(("replica", "shard"), None),
            P(("replica", "shard"), None),
            P(("replica", "shard"), None),
            P("shard", None),
            P("shard", None),
            P("shard", None),
            P("shard"),
            P("shard"),
            P("shard", None),
            P("shard", None, "replica"),
            P("shard", "replica", None),
        ),
        out_specs=(
            P(("replica", "shard"), None),
            P(("replica", "shard"), None),
            P("shard", None),
            P("shard", None),
            P("shard", None),
            P("shard"),
            P("shard"),
            P("shard", None),
            P("shard", None, "replica"),
            P("shard", "replica", None),
        ),
        check_vma=False,
    )
```

```python
import math

import jax
import jax.numpy as jnp
from jax import lax
from jax.experimental import pallas as pl
from jax.experimental.pallas import tpu as pltpu
from jax.sharding import PartitionSpec as P

CAP = 5
BLOCK = 128
VMEM_LIMIT = 60 * 1024 * 1024

bucket_edges = list(range(1, 16)) + [
    int(math.ceil(16.0 * 8.0 ** (step_m / 16.0))) for step_m in range(16)
]
epsilon = 1e-06
negative = -1e30
f32 = jnp.float32
bf16 = jnp.bfloat16


def dot(left, right, left_axis=1, right_axis=0, precision=None):
    return lax.dot_general(
        left,
        right,
        (((left_axis,), (right_axis,)), ((), ())),
        precision=precision,
        preferred_element_type=f32,
    )


def swap(values, axis, bit):
    count = lax.axis_size(axis)
    return lax.ppermute(values, axis, [(i, i ^ bit) for i in range(count)])


def bits_of(count):
    return [1 << i for i in reversed(range(count.bit_length() - 1))]


def add_half(left, right):
    if left.dtype == f32:
        return left + right
    return (left.astype(f32) + right.astype(f32)).astype(left.dtype)


def exchange(blocks):
    return [blocks[0]] + [swap(blocks[k], "shard", k) for k in range(1, len(blocks))]


def after(values, *others):
    return lax.optimization_barrier((values, others))[0]


def widen(values, bit):
    return jnp.concatenate([values, swap(values, "replica", bit)], axis=1)


def narrow(values, bit):
    half = values.shape[1] // 2
    return add_half(values[:, :half], swap(values[:, half:], "replica", bit))


def absolute(values, me, count):
    bit = 1
    shape = values.shape
    while bit < count:
        pairs = values.reshape((count // (2 * bit), 2, bit) + shape[1:])
        flipped = jnp.concatenate([pairs[:, 1:], pairs[:, :1]], axis=1)
        values = jnp.where((me & bit) != 0, flipped, pairs).reshape(shape)
        bit *= 2
    return values


def gather_pieces(values, order):
    me = lax.axis_index("replica")
    held = values[None]
    for bit in order:
        other = swap(held, "replica", bit)
        upper = (me & bit) != 0
        held = jnp.stack([jnp.where(upper, other, held), jnp.where(upper, held, other)], axis=0)
        held = held.reshape((-1,) + values.shape)
    bits = len(order)
    held = held.reshape((2,) * bits + values.shape)
    axes = [bits - 1 - order.index(b) for b in sorted(order, reverse=True)]
    held = jnp.transpose(held, [bits] + axes + [bits + 1, bits + 2])
    return held.reshape((values.shape[0], -1) + values.shape[1:])


def reduce_rows(values):
    me = lax.axis_index("replica")
    count = values.shape[0]
    bit = 1
    while bit < count:
        pairs = values.reshape((values.shape[0] // 2, 2) + values.shape[1:])
        low, high = pairs[:, 0], pairs[:, 1]
        upper = (me & bit) != 0
        values = add_half(
            jnp.where(upper, high, low), swap(jnp.where(upper, low, high), "replica", bit)
        )
        bit *= 2
    return values[0]


def near_tiles(block_count):
    return [d for d in range(block_count) if BLOCK * d - (BLOCK - 1) < bucket_edges[-1]]


def tile_distance(d):
    row = lax.broadcasted_iota(jnp.int32, (BLOCK, BLOCK), 0)
    col = lax.broadcasted_iota(jnp.int32, (BLOCK, BLOCK), 1)
    return row - col + BLOCK * d


def bias_row(table_ref, head, block, near, tiles):
    parts = []
    for j in range(block + 1):
        d = block - j
        if d < near:
            parts.append(tiles[d])
        else:
            parts.append(
                jnp.full((BLOCK, BLOCK), table_ref[len(bucket_edges), head], f32)
            )
    return parts[0] if len(parts) == 1 else jnp.concatenate(parts, axis=1)


def bias_tiles(table_ref, head, near):
    tiles = []
    for d in range(near):
        dist = tile_distance(d)
        tile = jnp.full((BLOCK, BLOCK), table_ref[0, head], f32)
        for index, edge in enumerate(bucket_edges):
            if edge > BLOCK * d + BLOCK - 1:
                break
            tile = jnp.where(dist >= edge, table_ref[index + 1, head], tile)
        if d == 0:
            tile = jnp.where(dist >= 0, tile, negative)
        tiles.append(tile)
    return tiles


def attention_forward(heads_here, head_dim, qscale, shards, me_ref, table_ref, *refs):
    token_refs, (gain_ref, full_ref) = refs[:shards], refs[shards : shards + 2]
    x_ref, n1_ref, qkv_ref, o_ref, lse_ref = refs[shards + 2 : shards + 7]
    ob_refs = refs[shards + 7 : 2 * shards + 7]
    ob_all = refs[-1]
    me = me_ref[0]
    tok_rows = token_refs[0].shape[0]
    for k in range(shards):
        x_ref[pl.ds((me ^ k) * tok_rows, tok_rows), :] = token_refs[k][...]
    seq = x_ref.shape[0]
    blocks = seq // BLOCK
    near = len(near_tiles(blocks))
    x = x_ref[...].astype(f32)
    inv = lax.rsqrt(jnp.mean(x * x, axis=1, keepdims=True) + epsilon)
    n1_ref[...] = (x * inv * gain_ref[...]).astype(bf16)
    wide = 3 * head_dim
    base = full_ref.shape[1] - heads_here * wide
    for h in range(heads_here):
        projected = dot(n1_ref[...], full_ref[:, base + h * wide : base + (h + 1) * wide])
        query = (projected[:, :head_dim] * qscale).astype(bf16)
        key = projected[:, head_dim : 2 * head_dim].astype(bf16)
        value = projected[:, 2 * head_dim :].astype(bf16)
        qkv_ref[h, :, :] = jnp.concatenate([query, key, value], axis=1)
        tiles = bias_tiles(table_ref, h, near)
        for i in range(blocks):
            span = (i + 1) * BLOCK
            rows = slice(i * BLOCK, span)
            scores = dot(query[rows], key[:span], 1, 1) + bias_row(table_ref, h, i, near, tiles)
            peak = jnp.max(scores, axis=1, keepdims=True)
            weights = jnp.exp(scores - peak)
            total = jnp.sum(weights, axis=1, keepdims=True)
            weights = (weights * (1.0 / total)).astype(bf16)
            attended = dot(weights, value[:span])
            o_ref[h, rows, :] = attended
            ob_all[rows, h * head_dim : (h + 1) * head_dim] = attended.astype(bf16)
            lse_ref[h, rows, :] = jnp.broadcast_to(peak + jnp.log(total), (BLOCK, BLOCK))
    for k in range(shards):
        ob_refs[k][...] = ob_all[pl.ds((me ^ k) * tok_rows, tok_rows), :]


def attention_backward(heads_here, head_dim, qscale, shards, me_ref, table_ref, x_ref, n1_ref,
                       qkv_ref, o_ref, lse_ref, full_ref, *refs):
    do_refs = refs[:shards]
    gw_ref, gain_ref, tab_ref = refs[shards : shards + 3]
    dn1_refs = refs[shards + 3 : 2 * shards + 3]
    dk_ref, dv_ref, dq_ref, acc_ref, do_ref = refs[2 * shards + 3 :]
    me = me_ref[0]
    tok_rows = do_refs[0].shape[0]
    for k in range(shards):
        do_ref[pl.ds((me ^ k) * tok_rows, tok_rows), :] = do_refs[k][...]
    seq = x_ref.shape[0]
    blocks = seq // BLOCK
    near = len(near_tiles(blocks))
    wide = 3 * head_dim
    base = full_ref.shape[1] - heads_here * wide
    bucket_count = len(bucket_edges) + 1
    for h in range(heads_here):
        query = qkv_ref[h, :, :head_dim]
        key = qkv_ref[h, :, head_dim : 2 * head_dim]
        value = qkv_ref[h, :, 2 * head_dim :]
        grad = do_ref[:, h * head_dim : (h + 1) * head_dim]
        tiles = bias_tiles(table_ref, h, near)
        sums = [jnp.zeros((BLOCK, BLOCK), f32) for _ in range(near + 1)]
        dk_ref[...] = jnp.zeros_like(dk_ref)
        dv_ref[...] = jnp.zeros_like(dv_ref)
        for i in range(blocks):
            span = (i + 1) * BLOCK
            rows = slice(i * BLOCK, span)
            q_i, g_i = query[rows], grad[rows]
            scores = dot(q_i, key[:span], 1, 1) + bias_row(table_ref, h, i, near, tiles)
            weights = jnp.exp(scores - lse_ref[h, rows, :][:, :1])
            delta = jnp.sum(g_i.astype(f32) * o_ref[h, rows, :], axis=1, keepdims=True)
            grad_scores = weights * (dot(g_i, value[:span], 1, 1) - delta)
            for j in range(i + 1):
                d = min(i - j, near)
                sums[d] = sums[d] + grad_scores[:, j * BLOCK : (j + 1) * BLOCK]
            half = grad_scores.astype(bf16)
            dq_ref[rows, :] = dot(half, key[:span])
            dk_ref[:span, :] += dot(half, q_i, 0, 0)
            dv_ref[:span, :] += dot(weights.astype(bf16), g_i, 0, 0)
        for b in range(bucket_count):
            low = 0 if b == 0 else bucket_edges[b - 1]
            high = bucket_edges[b] if b < len(bucket_edges) else None
            total = jnp.zeros((1, BLOCK), f32)
            for d in range(near):
                if BLOCK * d + BLOCK - 1 < low:
                    continue
                if high is not None and BLOCK * d - (BLOCK - 1) >= high:
                    continue
                dist = tile_distance(d)
                inside = dist >= low
                if high is not None:
                    inside = inside & (dist < high)
                total = total + jnp.sum(jnp.where(inside, sums[d], 0.0), axis=0, keepdims=True)
            if high is None:
                total = total + jnp.sum(sums[near], axis=0, keepdims=True)
            tab_ref[h, b : b + 1, :] = total
        projected = jnp.concatenate(
            [
                (dq_ref[...] * qscale).astype(bf16),
                dk_ref[...].astype(bf16),
                dv_ref[...].astype(bf16),
            ],
            axis=1,
        )
        gw_ref[:, h * wide : (h + 1) * wide] = dot(n1_ref[...], projected, 0, 0).astype(bf16)
        part = dot(projected, full_ref[:, base + h * wide : base + (h + 1) * wide], 1, 1)
        if h == 0:
            acc_ref[...] = part
        else:
            acc_ref[...] += part
    x = x_ref[...].astype(f32)
    inv = lax.rsqrt(jnp.mean(x * x, axis=1, keepdims=True) + epsilon)
    gain_ref[...] = jnp.sum(acc_ref[...] * x * inv, axis=0, keepdims=True)
    for k in range(shards):
        dn1_refs[k][...] = acc_ref[pl.ds((me ^ k) * tok_rows, tok_rows), :].astype(bf16)


def lane_value(values, lane, index):
    return jnp.sum(jnp.where(lane == index, values, 0.0), axis=1, keepdims=True)


def middle_forward(shards, dense_rows, width, me_ref, x_ref, routes_ref, place_ref, gain_ref,
                   full_ref, *refs):
    ob_refs = refs[:shards]
    hidden_ref, gates_ref, placed_ref = refs[shards:]
    me = me_ref[0]
    total = x_ref[...].astype(f32)
    for k in range(shards):
        total = total + dot(
            ob_refs[k][:, :dense_rows],
            full_ref[pl.ds((me ^ k) * dense_rows, dense_rows), :width],
        )
    hidden_ref[...] = total
    inv = lax.rsqrt(jnp.mean(total * total, axis=1, keepdims=True) + epsilon)
    normed = (total * inv * gain_ref[...]).astype(bf16)
    logits = dot(normed, full_ref[:, width:])
    lane = lax.broadcasted_iota(jnp.int32, logits.shape, 1)
    margin = lane_value(logits, lane, routes_ref[:, :1]) - lane_value(
        logits, lane, routes_ref[:, 1:2]
    )
    gates_ref[...] = jnp.where(
        lane == 0, jax.nn.sigmoid(margin), jnp.where(lane == 1, jax.nn.sigmoid(-margin), 0.0)
    )
    placed_ref[...] = dot(place_ref[...], normed).astype(bf16)


def middle_backward(shards, dense_rows, width, me_ref, hidden_ref, g_ref, place_ref, gain_ref,
                    full_ref, *refs):
    ob_refs, dx_refs = refs[:shards], refs[shards : 2 * shards]
    gh_ref, gain_out_ref, go_ref = refs[2 * shards : 2 * shards + 3]
    do_refs = refs[2 * shards + 3 :]
    me = me_ref[0]
    count = dx_refs[0].shape[0]
    hidden = hidden_ref[...]
    normed = jnp.zeros_like(hidden)
    for k in range(shards):
        normed = normed + dot(place_ref[k * count : (k + 1) * count, :], dx_refs[k][...], 0, 0)
    inv = lax.rsqrt(jnp.mean(hidden * hidden, axis=1, keepdims=True) + epsilon)
    weighted = normed * gain_ref[...]
    grad = (
        g_ref[...].astype(f32)
        + inv * weighted
        - hidden * (inv * inv * inv) * jnp.mean(weighted * hidden, axis=1, keepdims=True)
    )
    gh_ref[...] = grad
    gain_out_ref[...] = jnp.sum(normed * hidden * inv, axis=0, keepdims=True)
    branch = grad.astype(bf16)
    for k in range(shards):
        rows = full_ref[pl.ds((me ^ k) * dense_rows, dense_rows), :width]
        part = dot(branch, rows, 1, 1).astype(bf16)
        spare = do_refs[k].shape[1] - dense_rows
        if spare:
            part = jnp.concatenate([part, jnp.zeros((part.shape[0], spare), bf16)], axis=1)
        do_refs[k][...] = part
        go_ref[k, :, :] = dot(ob_refs[k][:, :dense_rows], branch, 0, 0).astype(bf16)


def expert_step(first, local, width, me_ref, x0_ref, x1_ref, g0_ref, g1_ref, router_ref,
                win_ref, wout_ref, *refs):
    dx0_ref, dx1_ref, y0_ref, y1_ref, gr_ref, gwin_ref, gwout_ref = refs[-7:]
    step = pl.program_id(0)
    expert = me_ref[0] * local + first + step
    x = jnp.concatenate([x0_ref[0], x1_ref[0]], axis=0)
    g_wide = jnp.concatenate([g0_ref[0], g1_ref[0]], axis=0)
    g = g_wide[:, :width]
    partner = g_wide[:, width : width + 1].astype(f32).astype(jnp.int32)
    w_in = win_ref[0]
    w_out = wout_ref[0]
    router = router_ref[...]
    rows = x0_ref.shape[1]
    logits = dot(x, router)
    lane = lax.broadcasted_iota(jnp.int32, logits.shape, 1)
    margin = lane_value(logits, lane, expert) - lane_value(logits, lane, partner)
    gate = jax.nn.sigmoid(margin)
    pre = dot(x, w_in)
    c0 = math.sqrt(2.0 / math.pi)
    square = pre * pre
    bent = jnp.tanh(c0 * (pre + 0.044715 * (square * pre)))
    act = (0.5 * pre * (1.0 + bent)).astype(bf16)
    slope = 0.5 * (1.0 + bent) + 0.5 * pre * (1.0 - bent * bent) * (
        c0 * (1.0 + 3.0 * 0.044715 * square)
    )
    back = dot(g, w_out, 1, 1)
    scaled = (gate * g.astype(f32)).astype(bf16)
    dgate = jnp.sum(act.astype(f32) * back, axis=1, keepdims=True)
    pull = gate * jax.nn.sigmoid(-margin) * dgate
    pull = jnp.where(lane == expert, pull, 0.0) - jnp.where(lane == partner, pull, 0.0)
    pull_high = pull.astype(bf16)
    pull_low = (pull - pull_high.astype(f32)).astype(bf16)
    dpre = (gate * back * slope).astype(bf16)
    dx = dot(dpre, w_in, 1, 1) + dot(pull_high, router, 1, 1) + dot(pull_low, router, 1, 1)
    dx = dx.astype(bf16)
    dx0_ref[0] = dx[:rows]
    dx1_ref[0] = dx[rows:]
    y = dot(act, w_out).astype(bf16)
    y0_ref[0] = y[:rows]
    y1_ref[0] = y[rows:]
    part = dot(x, pull_high, 0, 0) + dot(x, pull_low, 0, 0)

    @pl.when(step == 0)
    def _():
        gr_ref[...] = part

    @pl.when(step != 0)
    def _():
        gr_ref[...] += part

    gwin_ref[0] = dot(x, dpre, 0, 0)
    gwout_ref[0] = dot(act, scaled, 0, 0)


def run_experts(first, me_shard, xs, gs, full, w_in, w_out, held):
    count, rows, width = xs[0].shape
    local, _, hidden = w_in.shape
    x_spec = pl.BlockSpec((1, rows, width), lambda e: (e, 0, 0))
    g_spec = pl.BlockSpec((1, rows, gs[0].shape[2]), lambda e: (e, 0, 0))
    router_spec = pl.BlockSpec((width, BLOCK), lambda e: (0, width // BLOCK))
    in_spec = pl.BlockSpec((1, width, hidden), lambda e: (e + first, 0, 0))
    out_spec = pl.BlockSpec((1, hidden, width), lambda e: (e + first, 0, 0))
    smem = pl.BlockSpec(memory_space=pltpu.SMEM)
    anywhere = pl.BlockSpec(memory_space=pl.ANY)
    return pl.pallas_call(
        lambda *refs: expert_step(first, local, width, *refs),
        grid=(count,),
        in_specs=[smem, x_spec, x_spec, g_spec, g_spec, router_spec, in_spec, out_spec]
        + [anywhere] * len(held),
        out_specs=[x_spec] * 4
        + [pl.BlockSpec((width, BLOCK), lambda e: (0, 0)), in_spec, out_spec],
        out_shape=[jax.ShapeDtypeStruct(xs[0].shape, bf16)] * 4
        + [
            jax.ShapeDtypeStruct((width, BLOCK), f32),
            jax.ShapeDtypeStruct(w_in.shape, f32),
            jax.ShapeDtypeStruct(w_out.shape, f32),
        ],
        input_output_aliases={8 + i: 5 + i for i in range(len(held))},
        compiler_params=pltpu.CompilerParams(
            dimension_semantics=("arbitrary",), vmem_limit_bytes=VMEM_LIMIT
        ),
        cost_estimate=pl.CostEstimate(
            flops=24 * count * rows * width * hidden,
            transcendentals=2 * count * rows * hidden,
            bytes_accessed=12 * count * width * hidden + 16 * count * rows * width,
        ),
        name="experts",
    )(me_shard, *xs, *gs, full, w_in, w_out, *held)


def body(
    tokens,
    cotangent,
    routes,
    qkv_weight,
    out_weight,
    router_weight,
    attn_gain,
    moe_gain,
    bias_table,
    expert_in,
    expert_out,
):
    shards = lax.axis_size("shard")
    replicas = lax.axis_size("replica")
    me_shard = lax.axis_index("shard")
    me_replica = lax.axis_index("replica")
    me_array = me_shard.astype(jnp.int32).reshape(1)
    tok_rows, width = tokens.shape
    seq_len = tok_rows * shards
    table_rows, head_count = bias_table.shape
    bucket_count = table_rows * shards
    head_dim = width // head_count
    heads_here = -(-head_count // shards)
    head_pad = heads_here * shards - head_count
    wide = 3 * head_dim
    columns_here = heads_here * head_dim
    experts = router_weight.shape[1]
    local = expert_in.shape[0]
    dense_rows = width // shards
    piece = dense_rows // replicas
    qscale = 1.0 / math.sqrt(head_dim)
    order_a = bits_of(replicas)
    order_b = order_a[:-1][::-1] + order_a[-1:]
    core = order_a[-1]
    block_slots = CAP * local
    slot_count = experts * CAP
    half_local = local // 2

    hits = routes[:, :, None] == lax.iota(jnp.int32, experts)[None, None, :]
    named = (hits[:, 0] | hits[:, 1]).astype(bf16)
    earlier = (
        lax.iota(jnp.int32, tok_rows)[:, None] > lax.iota(jnp.int32, tok_rows)[None, :]
    ).astype(bf16)
    prior = dot(earlier, named)
    rank = jnp.sum(jnp.where(hits, prior[:, None, :], 0.0), axis=2).astype(jnp.int32)
    slot = ((routes // local) ^ me_shard) * block_slots + rank * local + routes % local
    slot_iota = lax.iota(jnp.int32, slot_count)
    place = [(slot_iota[:, None] == slot[None, :, k]).astype(bf16) for k in range(2)]
    place_any = place[0] + place[1]
    row_expert = slot_iota // (shards * CAP)
    row_source = (
        (slot_iota % (shards * CAP)) // CAP * block_slots + slot_iota % CAP * local + row_expert
    )
    to_expert = (slot_iota[None, :] == row_source[:, None]).astype(bf16)

    def blocks_of(values):
        return [values[k * block_slots : (k + 1) * block_slots] for k in range(shards)]

    def expert_major(blocks):
        rows = dot(to_expert, jnp.concatenate(blocks, axis=0)).astype(bf16)
        rows = rows.reshape(local, shards * CAP, rows.shape[1])
        return rows[:half_local], rows[half_local:]

    def slot_blocks(first, second):
        rows = jnp.concatenate([first, second], axis=0).reshape(slot_count, width)
        return blocks_of(dot(to_expert, rows, 0, 0).astype(bf16))

    small = jnp.concatenate(
        [
            router_weight,
            attn_gain[:, None],
            moe_gain[:, None],
            jnp.zeros((dense_rows, BLOCK - experts - 2), bf16),
        ],
        axis=1,
    )
    common = lax.dynamic_slice_in_dim(
        jnp.concatenate([out_weight, small], axis=1), me_replica * piece, piece, 0
    )
    columns = lax.dynamic_slice_in_dim(qkv_weight, me_replica * piece, piece, 0)
    columns = columns.reshape(piece, 3, head_count, head_dim)
    columns = jnp.pad(columns, ((0, 0), (0, 0), (0, head_pad), (0, 0)))
    columns = columns.reshape(piece, 3, shards, heads_here, head_dim)
    columns = jnp.transpose(columns, (2, 0, 3, 1, 4)).reshape(shards, piece, heads_here * wide)
    table_pad = jnp.pad(bias_table, ((0, 0), (0, head_pad)))
    table_pad = table_pad.reshape(table_rows, shards, heads_here)
    table_pad = jnp.swapaxes(table_pad, 0, 1).reshape(shards, table_rows * heads_here)
    table_pad = jnp.pad(table_pad, ((0, 0), (0, dense_rows - table_rows * heads_here)))
    table_piece = lax.dynamic_slice_in_dim(table_pad, me_replica * piece, piece, 1)
    lane = lax.iota(jnp.int32, width + BLOCK)
    dense = []
    for k in range(shards):
        target = me_shard ^ k
        table_column = lax.dynamic_index_in_dim(table_piece, target, 0, keepdims=False)
        shared = jnp.where(lane[None, :] == width + experts + 2, table_column[:, None], common)
        own = lax.dynamic_index_in_dim(columns, target, 0, keepdims=False)
        dense.append(jnp.concatenate([shared, own], axis=1))
    dense = exchange(dense)
    token_blocks = exchange([tokens] * shards)
    dense = absolute(jnp.stack(dense, axis=0), me_shard, shards)
    split = shards // 2
    full = jnp.concatenate(
        [gather_pieces(dense[:split], order_a), gather_pieces(dense[split:], order_b)], axis=0
    ).reshape(width, width + BLOCK + heads_here * wide)
    gain_one = full[:, width + experts].astype(f32)[None, :]
    gain_two = full[:, width + experts + 1].astype(f32)[None, :]
    table_here = (
        full[:, width + experts + 2]
        .reshape(shards, dense_rows)[:, : table_rows * heads_here]
        .reshape(bucket_count, heads_here)
        .astype(f32)
    )

    partner = jnp.sum(
        place[0].astype(f32) * routes[None, :, 1].astype(f32)
        + place[1].astype(f32) * routes[None, :, 0].astype(f32),
        axis=1,
    )
    grad_blocks = dot(place_any, cotangent).astype(bf16)
    partner = jnp.where(lax.iota(jnp.int32, BLOCK)[None, :] == 0, partner[:, None], 0.0)
    grad_blocks = jnp.concatenate([grad_blocks, partner.astype(bf16)], axis=1)
    grad_blocks = exchange(blocks_of(grad_blocks))
    grad_a, grad_b = expert_major(grad_blocks)

    smem = pl.BlockSpec(memory_space=pltpu.SMEM)
    vmem = pl.BlockSpec(memory_space=pltpu.VMEM)
    params = pltpu.CompilerParams(vmem_limit_bytes=VMEM_LIMIT)
    attn_flops = heads_here * seq_len * (2 * width * wide + 2 * seq_len * head_dim)
    sequence, normed_one, qkv_rows, attended, log_total, *attended_b = pl.pallas_call(
        lambda *refs: attention_forward(heads_here, head_dim, qscale, shards, *refs),
        in_specs=[smem, smem] + [vmem] * (shards + 2),
        out_specs=[vmem] * (5 + shards),
        out_shape=[
            jax.ShapeDtypeStruct((seq_len, width), bf16),
            jax.ShapeDtypeStruct((seq_len, width), bf16),
            jax.ShapeDtypeStruct((heads_here, seq_len, wide), bf16),
            jax.ShapeDtypeStruct((heads_here, seq_len, head_dim), f32),
            jax.ShapeDtypeStruct((heads_here, seq_len, BLOCK), f32),
        ]
        + [jax.ShapeDtypeStruct((tok_rows, columns_here), bf16)] * shards,
        scratch_shapes=[pltpu.VMEM((seq_len, columns_here), bf16)],
        compiler_params=params,
        cost_estimate=pl.CostEstimate(
            flops=attn_flops,
            transcendentals=heads_here * seq_len * seq_len,
            bytes_accessed=8 * seq_len * width,
        ),
        name="attention_forward",
    )(me_array, table_here, *token_blocks, gain_one, after(full, grad_a, grad_b))
    grad_a, grad_b = widen(grad_a, order_a[0]), widen(grad_b, order_b[0])
    attended_b = after(attended_b, grad_a, grad_b)
    attended_b = exchange(attended_b)
    for i in range(1, len(order_a) - 1):
        grad_a, grad_b = widen(grad_a, order_a[i]), widen(grad_b, order_b[i])

    shared_spec = pl.BlockSpec((width, width + BLOCK), lambda i: (0, 0))

    def whole(shape):
        return pl.BlockSpec(shape, lambda i: (0,) * len(shape))

    hidden, gates, placed = pl.pallas_call(
        lambda *refs: middle_forward(shards, dense_rows, width, *refs),
        grid=(1,),
        in_specs=[
            smem,
            whole((tok_rows, width)),
            whole((tok_rows, 2)),
            whole((slot_count, tok_rows)),
            whole((1, width)),
            shared_spec,
        ]
        + [whole((tok_rows, columns_here))] * shards,
        out_specs=[
            whole((tok_rows, width)),
            whole((tok_rows, BLOCK)),
            whole((slot_count, width)),
        ],
        out_shape=[
            jax.ShapeDtypeStruct((tok_rows, width), f32),
            jax.ShapeDtypeStruct((tok_rows, BLOCK), f32),
            jax.ShapeDtypeStruct((slot_count, width), bf16),
        ],
        compiler_params=params,
        cost_estimate=pl.CostEstimate(
            flops=2 * tok_rows * width * width,
            transcendentals=tok_rows,
            bytes_accessed=2 * width * width,
        ),
        name="middle_forward",
    )(me_array, tokens, routes, place_any, gain_two, full, *attended_b)

    placed = after(placed, grad_a, grad_b)
    x_a, x_b = expert_major(exchange(blocks_of(placed)))
    grad_a, grad_b = [(g, swap(g, "replica", core)) for g in (grad_a, grad_b)]
    x_a, x_b = widen(x_a, order_a[0]), widen(x_b, order_b[0])
    x_a, x_b, grad_a, grad_b = lax.optimization_barrier((x_a, x_b, grad_a, grad_b))
    for i in range(1, len(order_a) - 1):
        x_a, x_b = widen(x_a, order_a[i]), widen(x_b, order_b[i])
    x_a, x_b = [(x, swap(x, "replica", core)) for x in (x_a, x_b)]

    *rows_a, router_a, grad_in, grad_out = run_experts(
        0, me_array, x_a, grad_a, full, expert_in, expert_out, ()
    )
    *rows_b, router_b, grad_expert_in, grad_expert_out = run_experts(
        half_local, me_array, x_b, grad_b, full, expert_in, expert_out, (grad_in, grad_out)
    )

    def bring(first, second):
        held = [add_half(v[0], swap(v[1], "replica", core)) for v in (first, second)]
        for i in reversed(range(len(order_a) - 1)):
            held = [narrow(v, o[i]) for v, o in zip(held, (order_a, order_b))]
        return exchange(slot_blocks(*held))

    dx_blocks = bring(rows_a[:2], rows_b[:2])

    grad_hidden, grad_gain_two, grad_out_blocks, *grad_att = pl.pallas_call(
        lambda *refs: middle_backward(shards, dense_rows, width, *refs),
        grid=(1,),
        in_specs=[
            smem,
            whole((tok_rows, width)),
            whole((tok_rows, width)),
            whole((slot_count, tok_rows)),
            whole((1, width)),
            shared_spec,
        ]
        + [whole((tok_rows, columns_here))] * shards
        + [whole((block_slots, width))] * shards,
        out_specs=[
            whole((tok_rows, width)),
            whole((1, width)),
            whole((shards, dense_rows, width)),
        ]
        + [whole((tok_rows, columns_here))] * shards,
        out_shape=[
            jax.ShapeDtypeStruct((tok_rows, width), f32),
            jax.ShapeDtypeStruct((1, width), f32),
            jax.ShapeDtypeStruct((shards, dense_rows, width), bf16),
        ]
        + [jax.ShapeDtypeStruct((tok_rows, columns_here), bf16)] * shards,
        compiler_params=params,
        cost_estimate=pl.CostEstimate(
            flops=4 * tok_rows * width * width,
            transcendentals=tok_rows,
            bytes_accessed=2 * width * width,
        ),
        name="middle_backward",
    )(me_array, hidden, cotangent, place_any, gain_two, full, *attended_b, *dx_blocks)
    grad_att = exchange(grad_att)

    extra = jnp.where(
        lax.iota(jnp.int32, BLOCK)[None, :] == experts,
        grad_gain_two.reshape(width, 1),
        router_a + router_b,
    ).astype(bf16)
    extra = jnp.stack(
        [
            lax.dynamic_slice_in_dim(extra, (me_shard ^ k) * dense_rows, dense_rows, 0)
            for k in range(shards)
        ],
        axis=0,
    )

    def by_replica(values):
        cols = values.shape[-1]
        values = jnp.swapaxes(values.reshape(shards, replicas, piece, cols), 0, 1)
        return reduce_rows(values.reshape(replicas, shards * piece, cols)).reshape(
            shards, piece, cols
        )

    dense_two = by_replica(jnp.concatenate([grad_out_blocks, extra], axis=2))
    dense_two = exchange([dense_two[k] for k in range(shards)])
    dense_two = sum(v.astype(f32) for v in dense_two).astype(bf16)
    dense_two = gather_pieces(dense_two[None], order_a).reshape(dense_rows, width + BLOCK)
    dense_two = dense_two.astype(f32)

    grad_qkv, gain_part, table_part, *grad_n1 = pl.pallas_call(
        lambda *refs: attention_backward(heads_here, head_dim, qscale, shards, *refs),
        in_specs=[smem, smem] + [vmem] * (6 + shards),
        out_specs=[vmem] * (3 + shards),
        out_shape=[
            jax.ShapeDtypeStruct((width, heads_here * wide), bf16),
            jax.ShapeDtypeStruct((1, width), f32),
            jax.ShapeDtypeStruct((heads_here, bucket_count, BLOCK), f32),
        ]
        + [jax.ShapeDtypeStruct((tok_rows, width), bf16)] * shards,
        scratch_shapes=[
            pltpu.VMEM((seq_len, head_dim), f32),
            pltpu.VMEM((seq_len, head_dim), f32),
            pltpu.VMEM((seq_len, head_dim), f32),
            pltpu.VMEM((seq_len, width), f32),
            pltpu.VMEM((seq_len, columns_here), bf16),
        ],
        compiler_params=params,
        cost_estimate=pl.CostEstimate(
            flops=3 * attn_flops,
            transcendentals=heads_here * seq_len * seq_len,
            bytes_accessed=8 * seq_len * width,
        ),
        name="attention_backward",
    )(
        me_array, table_here, sequence, normed_one, qkv_rows, attended, log_total, full, *grad_att
    )

    table_part = jnp.transpose(jnp.sum(table_part, axis=2))
    table_column = jnp.pad(
        table_part.reshape(shards, table_rows * heads_here),
        ((0, 0), (0, dense_rows - table_rows * heads_here)),
    )
    spare = -(heads_here * wide) % BLOCK
    spare = spare if spare >= 2 else spare + BLOCK
    lane = lax.iota(jnp.int32, spare)[None, :]
    extra = jnp.where(
        lane == 0,
        gain_part.reshape(width, 1),
        jnp.where(lane == 1, table_column.reshape(width, 1), 0.0),
    ).astype(bf16)
    dense_one = by_replica(jnp.concatenate([grad_qkv, extra], axis=1))
    dense_one = exchange(
        [
            lax.dynamic_index_in_dim(dense_one, me_shard ^ k, 0, keepdims=False)
            for k in range(shards)
        ]
    )
    grad_n1 = exchange(grad_n1)
    dense_one = absolute(jnp.stack(dense_one, axis=0), me_shard, shards)
    own_qkv = dense_one[:, :, : heads_here * wide].reshape(
        shards, piece, heads_here, 3, head_dim
    )
    own_qkv = jnp.transpose(own_qkv, (1, 3, 0, 2, 4)).reshape(piece, 3, -1)[:, :, :width]
    own_extra = dense_one[:, :, heads_here * wide :].astype(f32)
    own_gain = jnp.sum(own_extra[:, :, 0], axis=0)
    own_table = jnp.transpose(own_extra[:, :, 1])
    tail = jnp.concatenate(
        [own_gain[:, None], own_table, jnp.zeros((piece, BLOCK - 1 - shards), f32)], axis=1
    )
    final = jnp.concatenate([own_qkv.reshape(piece, 3 * width), tail.astype(bf16)], axis=1)
    final = lax.all_gather(final, "replica", axis=0, tiled=True).astype(f32)
    grad_qkv_weight = final[:, : 3 * width]
    final_one = final[:, 3 * width :]
    grad_attn_gain = final_one[:, 0]
    grad_table = final_one[: table_rows * heads_here, 1 : 1 + shards]
    grad_table = jnp.transpose(
        grad_table.reshape(table_rows, heads_here, shards), (0, 2, 1)
    ).reshape(table_rows, shards * heads_here)[:, :head_count]

    rows_a, rows_b = after((rows_a[2:], rows_b[2:]), grad_hidden)
    y_slots = jnp.concatenate(bring(rows_a, rows_b), axis=0)
    layer_out = hidden
    for k in range(2):
        layer_out = layer_out + gates[:, k : k + 1] * dot(place[k], y_slots, 0, 0)

    residual = tokens.astype(f32)
    inv_one = lax.rsqrt(jnp.mean(residual * residual, axis=-1, keepdims=True) + epsilon)
    weighted = sum(v.astype(f32) for v in grad_n1) * gain_one
    grad_tokens = (
        grad_hidden
        + inv_one * weighted
        - residual
        * (inv_one * inv_one * inv_one)
        * jnp.mean(weighted * residual, axis=-1, keepdims=True)
    )
    return (
        layer_out,
        grad_tokens,
        grad_qkv_weight,
        dense_two[:, :width],
        dense_two[:, width : width + experts],
        grad_attn_gain,
        dense_two[:, width + experts],
        grad_table,
        grad_expert_in,
        grad_expert_out,
    )


def solution(mesh):
    return jax.shard_map(
        body,
        mesh=mesh,
        in_specs=(
            P(("replica", "shard"), None),
            P(("replica", "shard"), None),
            P(("replica", "shard"), None),
            P("shard", None),
            P("shard", None),
            P("shard", None),
            P("shard"),
            P("shard"),
            P("shard", None),
            P("shard", None, "replica"),
            P("shard", "replica", None),
        ),
        out_specs=(
            P(("replica", "shard"), None),
            P(("replica", "shard"), None),
            P("shard", None),
            P("shard", None),
            P("shard", None),
            P("shard"),
            P("shard"),
            P("shard", None),
            P("shard", None, "replica"),
            P("shard", "replica", None),
        ),
        check_vma=False,
    )
```
